32 devices in a mesh: gx: 2 (over core), gy: 4 (over y, x), ga: 4 (over z).
Axes of the slice: x: 2, y: 2, z: 4, core: 2. Of those that a mesh axis runs over, the one named last changes fastest.
Arguments:
- concentration: float32 [12, 128, 2048], P(None, 'gx', ('gy', 'ga')), may hold values from 0 to 2
- velocity: float32 [2, 128, 2048], P(None, 'gx', ('gy', 'ga')), may hold values from -0.4 to 0.4, as said below
- solid_fraction: float32 [128, 2048], P('gx', ('gy', 'ga')), may hold values from 0 to 1
- diffusivity: float32 [12], replicated, may hold values from 0.02 to 0.1
- voxel_index: int32 [32, 2048], P(('gx', 'gy', 'ga')), may hold values from 0 to 8191, as said below
- voxel_counts: int32 [2, 16], P('gx'), may hold values from 1 to 2048, 8192 in all within a row
- in_weight: bfloat16 [13, 128], replicated, may hold values from -1.75 to 1.75
- in_bias: float32 [128], replicated, may hold values from -3 to 3
- mid_weight: bfloat16 [128, 128], replicated, may hold values from -0.5 to 0.5
- mid_bias: float32 [128], replicated, may hold values from -3 to 3
- out_weight: bfloat16 [128, 12], replicated, may hold values from -0.5 to 0.5
- out_bias: float32 [12], replicated, may hold values from -2 to 2
Outputs:
- final_concentration: float32 [12, 128, 2048], P(None, 'gx', ('gy', 'ga'))
The draws below stay inside these ranges and needn't reach their ends.
Inputs may be any that keep to these rules, and one draw needn't show every extreme that they name: velocity[0] lies in -0.4 to 0.4 and velocity[1] in -0.15 to 0.15. `voxel_index`: each row holds 2048 different cells of its tile, as flat indices row * 128 + column. `voxel_counts`: in each row the 16 counts sum to 8192, and the largest is 2048.
All inputs are finite; a program needn't handle non-finite values.
Results may differ from the reference program's by a relative error of at most 0.00067.
Values may be sent and summed in bfloat16 or wider, within the bound.
A program may use at most 64 MiB of HBM per device.

```python
import math
import jax
import jax.numpy as jnp
import numpy as np
from jax import lax

SPECIES = 12
FEATURES = 13
HID_UNITS = 128
TILE_ROWS = 64
TILE_COLS = 128
SUBSTEPS = 4
COUPLINGS = 16
VOX_CAP = 2048
TILE_BANDS = 2
GROUP_TILES = 16
TILES = 32
GROUP_VOX = 8192
TOTAL_VOX = 16384
GRID_ROWS = 128
GRID_COLS = 2048


def draw_velocity(key, part):
    key_rows, key_cols = jax.random.split(key)
    unit_rows = jax.random.uniform(key_rows, (GRID_ROWS, GRID_COLS), jnp.float32, -1.0, 1.0)
    unit_cols = jax.random.uniform(key_cols, (GRID_ROWS, GRID_COLS), jnp.float32, -1.0, 1.0)
    speed_rows = 0.25 + 0.15 * unit_rows
    speed_cols = 0.15 * unit_cols
    return jnp.stack([speed_rows, speed_cols])


def draw_voxel_index(key, part):
    tile_keys = jax.random.split(key, TILES)

    def one_tile(tile_key):
        return jax.random.permutation(tile_key, TILE_ROWS * TILE_COLS)[:VOX_CAP].astype(jnp.int32)
    return jax.vmap(one_tile)(tile_keys)


def level_of(stream_key, dims, shards, smallest, top_value):
    factor_of, own = 1.0, jax.random.fold_in(stream_key, 6)
    for axis_at, blocks in shards:
        steps = jnp.exp(jax.random.uniform(jax.random.fold_in(own, axis_at), (blocks,), jnp.float32, smallest / len(shards), top_value / len(shards)))
        factor_of = factor_of * jnp.repeat(steps, dims[axis_at] // blocks).reshape([-1 if axis == axis_at else 1 for axis in range(len(dims))])
    return factor_of


def split_up(amount, total, most, skew):
    weights = [(1 << 20) // math.isqrt(standing ** skew) + 1 for standing in range(2, amount + 1)]
    surplus, given = total - most - (amount - 1), [1] * (amount - 1)
    while surplus > 0:
        free = [i for i in range(amount - 1) if given[i] < most]
        pool, remaining = sum([weights[i] for i in free]), surplus
        for i in free:
            extra = min(most - given[i], max(1, remaining * weights[i] // pool), surplus)
            given[i] = given[i] + extra
            surplus = surplus - extra
    return np.array([most] + given)


def ragged(own_key, number_of, total, limit, slope):
    if number_of == 2:
        one = jax.random.randint(own_key, (), max(1, total - limit), min(limit, total - 1) + 1)
        return jnp.stack([one, total - one])
    sizes = jnp.asarray(split_up(number_of, total, limit, slope), jnp.int32)
    couples = (number_of - 1) // 2
    giver, receiver = sizes[1:1 + 2 * couples:2], sizes[2:2 + 2 * couples:2]
    slack = jnp.minimum(giver - 1, limit - receiver)
    moved = jax.random.randint(jax.random.fold_in(own_key, 1), (couples,), 0, 1 << 20) % (slack + 1)
    sizes = sizes.at[1:1 + 2 * couples:2].set(giver - moved).at[2:2 + 2 * couples:2].set(receiver + moved)
    return sizes[jax.random.permutation(jax.random.fold_in(own_key, 2), number_of)]


def noise(key, shape, spread, most, kind=jnp.bfloat16):
    values = jax.random.normal(key, shape, jnp.float32) * spread
    return jnp.minimum(jnp.maximum(values, -most), most).astype(kind)


def setup_inputs(seed: int = 0) -> dict:
    key_list = jax.random.split(jax.random.key(seed), 13)
    concentration = jnp.clip(2.0 * jax.random.uniform(key_list[0], (SPECIES, GRID_ROWS, GRID_COLS), jnp.float32) ** level_of(key_list[0], (SPECIES, GRID_ROWS, GRID_COLS), ((1, 2), (2, 16)), -0.2, 0.2), 0.0, 2.0)
    velocity = draw_velocity(jax.random.fold_in(key_list[12], 71), 0)
    solid_fraction = jnp.clip(1.0 * jax.random.uniform(key_list[2], (GRID_ROWS, GRID_COLS), jnp.float32) ** level_of(key_list[2], (GRID_ROWS, GRID_COLS), ((0, 2), (1, 16)), -0.2, 0.2), 0.0, 1.0)
    diffusivity = jnp.clip(jnp.exp(jax.random.uniform(key_list[3], (SPECIES,), jnp.float32, math.log(0.02), math.log(0.1))), 0.02, 0.1)
    voxel_index = draw_voxel_index(jax.random.fold_in(key_list[12], 71), 0)
    voxel_counts = jax.vmap(lambda own: ragged(own, GROUP_TILES, GROUP_VOX, VOX_CAP, 2))(jax.random.split(key_list[5], TILE_BANDS)).reshape((TILE_BANDS, GROUP_TILES)).astype(jnp.int32)
    in_weight = noise(key_list[6], (FEATURES, HID_UNITS), FEATURES ** -0.5, 1.75)
    in_bias = noise(key_list[7], (HID_UNITS,), 0.5, 3.0, jnp.float32)
    mid_weight = noise(key_list[8], (HID_UNITS, HID_UNITS), HID_UNITS ** -0.5, 0.5)
    mid_bias = noise(key_list[9], (HID_UNITS,), 0.5, 3.0, jnp.float32)
    out_weight = noise(key_list[10], (HID_UNITS, SPECIES), HID_UNITS ** -0.5, 0.5)
    out_bias = noise(key_list[11], (SPECIES,), 0.3, 2.0, jnp.float32)
    return dict(concentration=concentration, velocity=velocity, solid_fraction=solid_fraction, diffusivity=diffusivity, voxel_index=voxel_index, voxel_counts=voxel_counts, in_weight=in_weight, in_bias=in_bias, mid_weight=mid_weight, mid_bias=mid_bias, out_weight=out_weight, out_bias=out_bias)


def advance(padded, velocity, diffusivity):
    centre = padded[:, 1:-1, 1:-1]
    above_rows = padded[:, :-2, 1:-1]
    below_rows = padded[:, 2:, 1:-1]
    left_cols = padded[:, 1:-1, :-2]
    right_cols = padded[:, 1:-1, 2:]
    speed_rows = velocity[0]
    speed_cols = velocity[1]
    upwind = jnp.maximum(speed_rows, 0.0) * (centre - above_rows) + jnp.minimum(speed_rows, 0.0) * (below_rows - centre)
    upwind = upwind + jnp.maximum(speed_cols, 0.0) * (centre - left_cols) + jnp.minimum(speed_cols, 0.0) * (right_cols - centre)
    mixing = diffusivity[:, None, None] * ((above_rows + below_rows) + (left_cols + right_cols) - 4.0 * centre)
    return centre - upwind + mixing


def surrogate(features, in_weight, in_bias, mid_weight, mid_bias, out_weight, out_bias):
    layer_one = jnp.tanh(jnp.dot(features, in_weight, preferred_element_type=jnp.float32) + in_bias).astype(jnp.bfloat16)
    layer_two = jnp.tanh(jnp.dot(layer_one, mid_weight, preferred_element_type=jnp.float32) + mid_bias).astype(jnp.bfloat16)
    return (jnp.dot(layer_two, out_weight, preferred_element_type=jnp.float32) + out_bias).astype(jnp.bfloat16)


def reference(concentration, velocity, solid_fraction, diffusivity, voxel_index, voxel_counts, in_weight, in_bias, mid_weight, mid_bias, out_weight, out_bias):
    tile_number = jnp.arange(TILES, dtype=jnp.int32)
    tile_band = tile_number // GROUP_TILES
    tile_place = tile_number % GROUP_TILES
    rows_all = (tile_band[:, None] * TILE_ROWS + voxel_index // TILE_COLS).reshape(-1)
    cols_all = (tile_place[:, None] * TILE_COLS + voxel_index % TILE_COLS).reshape(-1)
    live_mask = (jnp.arange(VOX_CAP, dtype=jnp.int32)[None, :] < voxel_counts.reshape(TILES)[:, None]).reshape(-1)
    chosen = jnp.nonzero(live_mask, size=TOTAL_VOX)[0]
    rows_live = rows_all[chosen]
    cols_live = cols_all[chosen]
    solid_live = solid_fraction[rows_live, cols_live]

    def coupling(counter, state):
        for substep in range(SUBSTEPS):
            padded = jnp.pad(state, ((0, 0), (1, 1), (1, 1)))
            state = advance(padded, velocity, diffusivity)
        features = jnp.concatenate([state[:, rows_live, cols_live], solid_live[None, :]], axis=0).T.astype(jnp.bfloat16)
        increment = surrogate(features, in_weight, in_bias, mid_weight, mid_bias, out_weight, out_bias)
        increment = lax.optimization_barrier(increment).astype(jnp.float32)
        return state.at[:, rows_live, cols_live].add(increment.T)

    return lax.fori_loop(0, COUPLINGS, coupling, concentration)
```

```python
import jax
import jax.numpy as jnp
from jax import lax
from jax.experimental import pallas as pl
from jax.experimental.pallas import tpu as pltpu
from jax.sharding import PartitionSpec as P

SUBSTEPS = 4
COUPLINGS = 16
HALO = SUBSTEPS
SLOTS = 16
CHUNK = 8
MESH = pl.DeviceIdType.MESH


def kernel(
    rows, cols, species, gx_count, gy_count, ga_count,
    base_ref, vel_ref, diff_ref, index_ref, counts_ref, w1_ref, w2_ref, w3_ref,
    out_ref,
    state, other, coef_c, coef_u, coef_d, coef_l, coef_r, live,
    edge_out, top_out, bottom_out,
    from_left, from_right, from_up, from_down, from_corner,
    send_sem, recv_sem,
):
    full = rows + 2 * HALO
    width = 2 * HALO
    per_tile = cols // width
    tiles = rows // per_tile
    gx = lax.axis_index("gx")
    gy = lax.axis_index("gy")
    ga = lax.axis_index("ga")
    place = gy * ga_count + ga
    places = gy_count * ga_count

    def device(dx, dp):
        other_place = jnp.clip(place + dp, 0, places - 1)
        return (
            jnp.clip(gx + dx, 0, gx_count - 1),
            lax.div(other_place, ga_count),
            lax.rem(other_place, ga_count),
        )

    has_up, has_down = gx > 0, gx < gx_count - 1
    has_left, has_right = place > 0, place < places - 1
    links = (
        (device(0, -1), has_left),
        (device(0, 1), has_right),
        (device(-1, 0), has_up),
        (device(1, 0), has_down),
        (device(-1, -1), has_up & has_left),
        (device(1, 1), has_down & has_right),
        (device(-1, 1), has_up & has_right),
        (device(1, -1), has_down & has_left),
    )

    for ref in (from_left, from_right, from_up, from_down, from_corner):
        ref[...] = jnp.zeros_like(ref)

    barrier = pltpu.get_barrier_semaphore()
    total = jnp.int32(0)
    for target, exists in links:
        total = total + exists.astype(jnp.int32)

        @pl.when(exists)
        def _():
            pl.semaphore_signal(barrier, inc=1, device_id=target, device_id_type=MESH)

    pl.semaphore_wait(barrier, total)

    lane = lax.broadcasted_iota(jnp.int32, (SLOTS, cols), 1)
    sub = lax.broadcasted_iota(jnp.int32, (SLOTS, cols), 0)
    first_half = lax.rem(lane, width) < HALO

    def copies(slot):
        last = tiles - 1
        plan = (
            (edge_out, from_right.at[slot]),
            (edge_out, from_left.at[slot]),
            (top_out, from_down.at[slot]),
            (bottom_out, from_up.at[slot]),
            (edge_out.at[0], from_corner.at[slot, 3]),
            (edge_out.at[last], from_corner.at[slot, 0]),
            (edge_out.at[0], from_corner.at[slot, 2]),
            (edge_out.at[last], from_corner.at[slot, 1]),
        )
        result = []
        for at, ((source, target_ref), (target, exists)) in enumerate(zip(plan, links)):
            result.append((
                pltpu.make_async_remote_copy(
                    src_ref=source, dst_ref=target_ref,
                    send_sem=send_sem.at[at], recv_sem=recv_sem.at[slot, at],
                    device_id=target, device_id_type=MESH,
                ),
                exists,
            ))
        return result

    def start(slot):
        for tile in range(tiles):
            packed = jnp.zeros((SLOTS, cols), jnp.float32)
            for at in range(per_tile):
                row = state[HALO + tile * per_tile + at, :, 0:cols]
                moved = pltpu.roll(row, (width * at + HALO) % cols, axis=1)
                packed = moved if at == 0 else jnp.where(lane >= width * at, moved, packed)
            edge_out[tile] = packed
        top_out[...] = state[HALO : 2 * HALO, :, 0:cols]
        bottom_out[...] = state[rows : rows + HALO, :, 0:cols]
        for copy, exists in copies(slot):

            @pl.when(exists)
            def _():
                copy.start()

    def finish(slot, change):
        moves = copies(slot)
        for at, (copy, exists) in enumerate(moves):

            @pl.when(exists)
            def _():
                copy.wait_send()

            @pl.when(links[at ^ 1][1])
            def _():
                moves[at][0].wait_recv()

        edges = [
            jnp.where(first_half, from_left[slot, tile], from_right[slot, tile])
            for tile in range(tiles)
        ]
        corner_up = jnp.where(first_half, from_corner[slot, 0], from_corner[slot, 1])
        corner_down = jnp.where(first_half, from_corner[slot, 2], from_corner[slot, 3])
        corner = jnp.where(lane < width * HALO, corner_down, corner_up)
        blocks = edges + [corner]
        blocks += [from_up[slot, at] for at in range(HALO)]
        blocks += [from_down[slot, at] for at in range(HALO)]
        if change is not None:
            blocks = change(blocks)
        corner = blocks[tiles]
        for at in range(HALO):
            state[at, :, 0:cols] = blocks[tiles + 1 + at]
            state[HALO + rows + at, :, 0:cols] = blocks[tiles + 1 + HALO + at]
            window = per_tile - HALO + at
            state[at, :, cols : 2 * cols] = pltpu.roll(
                corner, (2 * cols - width * window - HALO) % cols, axis=1
            )
            state[HALO + rows + at, :, cols : 2 * cols] = pltpu.roll(
                corner, (2 * cols - width * at - HALO) % cols, axis=1
            )
        for tile in range(tiles):
            for at in range(per_tile):
                state[HALO + tile * per_tile + at, :, cols : 2 * cols] = pltpu.roll(
                    blocks[tile], (2 * cols - width * at - HALO) % cols, axis=1
                )

    def react(blocks):
        count = len(blocks)
        features = jnp.concatenate([block.astype(jnp.bfloat16) for block in blocks], axis=1)
        ones = jnp.ones((SLOTS, count * cols), jnp.bfloat16)
        hidden = jnp.dot(w1_ref[...], features, preferred_element_type=jnp.float32)
        hidden = jnp.tanh(hidden).astype(jnp.bfloat16)
        hidden = jnp.concatenate([hidden, ones], axis=0)
        hidden = jnp.dot(w2_ref[...], hidden, preferred_element_type=jnp.float32)
        hidden = jnp.tanh(hidden).astype(jnp.bfloat16)
        hidden = jnp.concatenate([hidden, ones], axis=0)
        gain = jnp.dot(w3_ref[...], hidden, preferred_element_type=jnp.float32)
        gain = gain.astype(jnp.bfloat16).astype(jnp.float32)
        return [
            block
            + jnp.where(
                jnp.broadcast_to(block[species + 1 : species + 2], block.shape) > 0.5,
                gain[:, at * cols : (at + 1) * cols],
                0.0,
            )
            for at, block in enumerate(blocks)
        ]

    @pl.loop(0, rows)
    def _(row):
        speed_rows = jnp.broadcast_to(vel_ref[0, pl.ds(row, 1), :], (SLOTS, cols))
        speed_cols = jnp.broadcast_to(vel_ref[1, pl.ds(row, 1), :], (SLOTS, cols))
        state[HALO + row, :, 0:cols] = jnp.where(
            sub == 0, speed_rows, jnp.where(sub == 1, speed_cols, 1.0)
        )

    start(0)

    candidates = index_ref[...]
    counts = counts_ref[...]
    own = lax.broadcasted_iota(jnp.int32, counts.shape, 1) == place
    own_count = jnp.sum(jnp.where(own, counts, 0), axis=1, keepdims=True)
    entry = lax.broadcasted_iota(jnp.int32, candidates.shape, 1)
    candidates = jnp.where(entry < own_count, candidates, -1)
    cell_row = jnp.right_shift(candidates, cols.bit_length() - 1)
    cell_col = jnp.bitwise_and(candidates, cols - 1)
    entries = candidates.shape[1]
    row_at = lax.broadcasted_iota(jnp.int32, (rows, entries), 0)
    col_at = lax.broadcasted_iota(jnp.int32, (cols, entries), 0)
    row_hot = jnp.where(row_at == cell_row, 1.0, 0.0).astype(jnp.bfloat16)
    col_hot = jnp.where(col_at == cell_col, 1.0, 0.0).astype(jnp.bfloat16)
    live[...] = lax.dot_general(
        row_hot, col_hot, (((1,), (1,)), ((), ())), preferred_element_type=jnp.float32
    )

    finish(0, None)
    sub2 = lax.broadcasted_iota(jnp.int32, (SLOTS, 2 * cols), 0)
    shares = diff_ref[...]
    spread = jnp.broadcast_to(shares, (SLOTS, 2 * cols))

    @pl.loop(0, full)
    def _(row):
        block = state[row]
        inside = jnp.where(sub2 < species, jnp.broadcast_to(block[2:3], block.shape), 0.0)
        speed_rows = jnp.broadcast_to(block[0:1], block.shape)
        speed_cols = jnp.broadcast_to(block[1:2], block.shape)
        coef_u[row] = inside * (jnp.maximum(speed_rows, 0.0) + spread)
        coef_d[row] = inside * (spread - jnp.minimum(speed_rows, 0.0))
        coef_l[row] = inside * (jnp.maximum(speed_cols, 0.0) + spread)
        coef_r[row] = inside * (spread - jnp.minimum(speed_cols, 0.0))
        coef_c[row] = 1.0 - inside * (
            jnp.abs(speed_rows) + jnp.abs(speed_cols) + 4.0 * spread
        )

    @pl.loop(0, rows)
    def _(row):
        flags = jnp.broadcast_to(live[pl.ds(row, 1), :], (SLOTS, cols))
        state[HALO + row, :, 0:cols] = jnp.where(sub == species + 1, flags, base_ref[row])

    start(1)
    finish(1, None)

    def substep(source, target, low, high):
        def body(row, carry):
            above, centre = carry
            below = source[row + 1]
            target[row] = (
                coef_c[row] * centre
                + coef_u[row] * above
                + coef_d[row] * below
                + coef_l[row] * pltpu.roll(centre, 1, axis=1)
                + coef_r[row] * pltpu.roll(centre, 2 * cols - 1, axis=1)
            )
            return centre, below

        lax.fori_loop(low, high, body, (source[low - 1], source[low]), unroll=2)

    @pl.loop(0, COUPLINGS)
    def _(step):
        for at in range(SUBSTEPS):
            source, target = (state, other) if at % 2 == 0 else (other, state)
            substep(source, target, at + 1, full - 1 - at)
        slot = lax.rem(step, 2)
        start(slot)

        @pl.loop(0, rows // CHUNK)
        def _(piece):
            first = HALO + piece * CHUNK
            blocks = react([state[first + at, :, 0:cols] for at in range(CHUNK)])
            for at in range(CHUNK):
                state[first + at, :, 0:cols] = blocks[at]

        finish(slot, react)

    out_ref[...] = state[HALO : HALO + rows, :, 0:cols]


def split_bias(bias):
    high = lax.reduce_precision(bias, 8, 7)
    return jnp.stack([high, bias - high], axis=1).astype(jnp.bfloat16)


def per_device(
    concentration, velocity, solid_fraction, diffusivity, voxel_index, voxel_counts,
    in_weight, in_bias, mid_weight, mid_bias, out_weight, out_bias,
):
    species, rows, cols = concentration.shape
    hidden = mid_weight.shape[0]
    base = jnp.concatenate(
        [
            jnp.transpose(concentration, (1, 0, 2)),
            solid_fraction[:, None, :],
            jnp.zeros((rows, 1, cols), jnp.float32),
            jnp.ones((rows, SLOTS - species - 2, cols), jnp.float32),
        ],
        axis=1,
    )
    shares = jnp.pad(diffusivity, (0, SLOTS - species))[:, None]
    w1 = jnp.concatenate(
        [in_weight.T, jnp.zeros((hidden, 1), jnp.bfloat16), split_bias(in_bias)], axis=1
    )
    gap = jnp.zeros((hidden, SLOTS - 2), jnp.bfloat16)
    w2 = jnp.concatenate([mid_weight.T, split_bias(mid_bias), gap], axis=1)
    w3 = jnp.concatenate([out_weight.T, split_bias(out_bias), gap[:species]], axis=1)
    w3 = jnp.pad(w3, ((0, SLOTS - species), (0, 0)))
    full = rows + 2 * HALO
    tiles = rows * 2 * HALO // cols
    sizes = [lax.axis_size(name) for name in ("gx", "gy", "ga")]

    def body(*refs):
        kernel(rows, cols, species, *sizes, *refs)

    whole = pltpu.VMEM((full, SLOTS, 2 * cols), jnp.float32)
    result = pl.pallas_call(
        body,
        out_shape=jax.ShapeDtypeStruct((rows, SLOTS, cols), jnp.float32),
        in_specs=[pl.BlockSpec(memory_space=pltpu.VMEM)] * 8,
        out_specs=pl.BlockSpec(memory_space=pltpu.VMEM),
        scratch_shapes=[whole] * 7
        + [
            pltpu.VMEM((rows, cols), jnp.float32),
            pltpu.VMEM((tiles, SLOTS, cols), jnp.float32),
            pltpu.VMEM((HALO, SLOTS, cols), jnp.float32),
            pltpu.VMEM((HALO, SLOTS, cols), jnp.float32),
            pltpu.VMEM((2, tiles, SLOTS, cols), jnp.float32),
            pltpu.VMEM((2, tiles, SLOTS, cols), jnp.float32),
            pltpu.VMEM((2, HALO, SLOTS, cols), jnp.float32),
            pltpu.VMEM((2, HALO, SLOTS, cols), jnp.float32),
            pltpu.VMEM((2, 4, SLOTS, cols), jnp.float32),
            pltpu.SemaphoreType.DMA((8,)),
            pltpu.SemaphoreType.DMA((2, 8)),
        ],
        compiler_params=pltpu.CompilerParams(
            collective_id=0, has_side_effects=True, vmem_limit_bytes=48 << 20
        ),
    )(base, velocity, shares, voxel_index, voxel_counts, w1, w2, w3)
    return jnp.transpose(result[:, :species, :], (1, 0, 2))


def solution(mesh):
    tile = P(None, "gx", ("gy", "ga"))
    return jax.shard_map(
        per_device,
        mesh=mesh,
        in_specs=(
            tile, tile, P("gx", ("gy", "ga")), P(),
            P(("gx", "gy", "ga"), None), P("gx", None),
            P(), P(), P(), P(), P(), P(),
        ),
        out_specs=tile,
        check_vma=False,
    )
```

```python
import jax
import jax.numpy as jnp
from jax import lax
from jax.experimental import pallas as pl
from jax.experimental.pallas import tpu as pltpu
from jax.sharding import PartitionSpec as P

SUBSTEPS = 4
COUPLINGS = 16
HALO = SUBSTEPS
SLOTS = 16
CHUNK = 8
GROUP = 10
MESH = pl.DeviceIdType.MESH


def kernel(
    rows, cols, species, gx_count, gy_count, ga_count,
    base_ref, vel_ref, diff_ref, index_ref, counts_ref, w1_ref, w2_ref, w3_ref,
    out_ref,
    state, other, coef_c, coef_u, coef_d, coef_l, coef_r, live,
    edge_out, top_out, bottom_out,
    from_left, from_right, from_up, from_down, from_corner,
    send_sem, recv_sem,
):
    full = rows + 2 * HALO
    width = 2 * HALO
    per_tile = cols // width
    tiles = rows // per_tile
    gx = lax.axis_index("gx")
    gy = lax.axis_index("gy")
    ga = lax.axis_index("ga")
    place = gy * ga_count + ga
    places = gy_count * ga_count

    def device(dx, dp):
        other_place = jnp.clip(place + dp, 0, places - 1)
        return (
            jnp.clip(gx + dx, 0, gx_count - 1),
            lax.div(other_place, ga_count),
            lax.rem(other_place, ga_count),
        )

    has_up, has_down = gx > 0, gx < gx_count - 1
    has_left, has_right = place > 0, place < places - 1
    links = (
        (device(0, -1), has_left),
        (device(0, 1), has_right),
        (device(-1, 0), has_up),
        (device(1, 0), has_down),
        (device(-1, -1), has_up & has_left),
        (device(1, 1), has_down & has_right),
        (device(-1, 1), has_up & has_right),
        (device(1, -1), has_down & has_left),
    )

    for ref in (from_left, from_right, from_up, from_down, from_corner):
        ref[...] = jnp.zeros_like(ref)

    barrier = pltpu.get_barrier_semaphore()
    total = jnp.int32(0)
    for target, exists in links:
        total = total + exists.astype(jnp.int32)

        @pl.when(exists)
        def _():
            pl.semaphore_signal(barrier, inc=1, device_id=target, device_id_type=MESH)

    pl.semaphore_wait(barrier, total)

    lane = lax.broadcasted_iota(jnp.int32, (SLOTS, cols), 1)
    sub = lax.broadcasted_iota(jnp.int32, (SLOTS, cols), 0)
    first_half = lax.rem(lane, width) < HALO

    def copies(slot):
        last = tiles - 1
        plan = (
            (edge_out, from_right.at[slot]),
            (edge_out, from_left.at[slot]),
            (top_out, from_down.at[slot]),
            (bottom_out, from_up.at[slot]),
            (edge_out.at[0], from_corner.at[slot, 3]),
            (edge_out.at[last], from_corner.at[slot, 0]),
            (edge_out.at[0], from_corner.at[slot, 2]),
            (edge_out.at[last], from_corner.at[slot, 1]),
        )
        result = []
        for at, ((source, target_ref), (target, exists)) in enumerate(zip(plan, links)):
            result.append((
                pltpu.make_async_remote_copy(
                    src_ref=source, dst_ref=target_ref,
                    send_sem=send_sem.at[at], recv_sem=recv_sem.at[slot, at],
                    device_id=target, device_id_type=MESH,
                ),
                exists,
            ))
        return result

    def start(slot):
        for tile in range(tiles):
            packed = jnp.zeros((SLOTS, cols), jnp.float32)
            for at in range(per_tile):
                row = state[HALO + tile * per_tile + at, :, 0:cols]
                moved = pltpu.roll(row, (width * at + HALO) % cols, axis=1)
                packed = moved if at == 0 else jnp.where(lane >= width * at, moved, packed)
            edge_out[tile] = packed
        top_out[...] = state[HALO : 2 * HALO, :, 0:cols]
        bottom_out[...] = state[rows : rows + HALO, :, 0:cols]
        for copy, exists in copies(slot):

            @pl.when(exists)
            def _():
                copy.start()

    def finish(slot, change):
        moves = copies(slot)
        for at, (copy, exists) in enumerate(moves):

            @pl.when(exists)
            def _():
                copy.wait_send()

            @pl.when(links[at ^ 1][1])
            def _():
                moves[at][0].wait_recv()

        edges = [
            jnp.where(first_half, from_left[slot, tile], from_right[slot, tile])
            for tile in range(tiles)
        ]
        corner_up = jnp.where(first_half, from_corner[slot, 0], from_corner[slot, 1])
        corner_down = jnp.where(first_half, from_corner[slot, 2], from_corner[slot, 3])
        corner = jnp.where(lane < width * HALO, corner_down, corner_up)
        blocks = edges + [corner]
        blocks += [from_up[slot, at] for at in range(HALO)]
        blocks += [from_down[slot, at] for at in range(HALO)]
        if change is not None:
            blocks = change(blocks)
        corner = blocks[tiles]
        for at in range(HALO):
            state[at, :, 0:cols] = blocks[tiles + 1 + at]
            state[HALO + rows + at, :, 0:cols] = blocks[tiles + 1 + HALO + at]
            window = per_tile - HALO + at
            state[at, :, cols : 2 * cols] = pltpu.roll(
                corner, (2 * cols - width * window - HALO) % cols, axis=1
            )
            state[HALO + rows + at, :, cols : 2 * cols] = pltpu.roll(
                corner, (2 * cols - width * at - HALO) % cols, axis=1
            )
        for tile in range(tiles):
            for at in range(per_tile):
                state[HALO + tile * per_tile + at, :, cols : 2 * cols] = pltpu.roll(
                    blocks[tile], (2 * cols - width * at - HALO) % cols, axis=1
                )

    def react(blocks):
        count = len(blocks)
        features = jnp.concatenate([block.astype(jnp.bfloat16) for block in blocks], axis=1)
        ones = jnp.ones((SLOTS, count * cols), jnp.bfloat16)
        hidden = jnp.dot(w1_ref[...], features, preferred_element_type=jnp.float32)
        hidden = jnp.tanh(hidden).astype(jnp.bfloat16)
        hidden = jnp.concatenate([hidden, ones], axis=0)
        hidden = jnp.dot(w2_ref[...], hidden, preferred_element_type=jnp.float32)
        hidden = jnp.tanh(hidden).astype(jnp.bfloat16)
        hidden = jnp.concatenate([hidden, ones], axis=0)
        gain = jnp.dot(w3_ref[...], hidden, preferred_element_type=jnp.float32)
        gain = gain.astype(jnp.bfloat16).astype(jnp.float32)
        return [
            block
            + jnp.where(
                jnp.broadcast_to(block[species + 1 : species + 2], block.shape) > 0.5,
                gain[:, at * cols : (at + 1) * cols],
                0.0,
            )
            for at, block in enumerate(blocks)
        ]

    @pl.loop(0, rows)
    def _(row):
        speed_rows = jnp.broadcast_to(vel_ref[0, pl.ds(row, 1), :], (SLOTS, cols))
        speed_cols = jnp.broadcast_to(vel_ref[1, pl.ds(row, 1), :], (SLOTS, cols))
        state[HALO + row, :, 0:cols] = jnp.where(
            sub == 0, speed_rows, jnp.where(sub == 1, speed_cols, 1.0)
        )

    start(0)

    candidates = index_ref[...]
    counts = counts_ref[...]
    own = lax.broadcasted_iota(jnp.int32, counts.shape, 1) == place
    own_count = jnp.sum(jnp.where(own, counts, 0), axis=1, keepdims=True)
    entry = lax.broadcasted_iota(jnp.int32, candidates.shape, 1)
    candidates = jnp.where(entry < own_count, candidates, -1)
    cell_row = jnp.right_shift(candidates, cols.bit_length() - 1)
    cell_col = jnp.bitwise_and(candidates, cols - 1)
    entries = candidates.shape[1]
    row_at = lax.broadcasted_iota(jnp.int32, (rows, entries), 0)
    col_at = lax.broadcasted_iota(jnp.int32, (cols, entries), 0)
    row_hot = jnp.where(row_at == cell_row, 1.0, 0.0).astype(jnp.bfloat16)
    col_hot = jnp.where(col_at == cell_col, 1.0, 0.0).astype(jnp.bfloat16)
    live[...] = lax.dot_general(
        row_hot, col_hot, (((1,), (1,)), ((), ())), preferred_element_type=jnp.float32
    )

    finish(0, None)
    sub2 = lax.broadcasted_iota(jnp.int32, (SLOTS, 2 * cols), 0)
    shares = diff_ref[...]
    spread = jnp.broadcast_to(shares, (SLOTS, 2 * cols))

    @pl.loop(0, full)
    def _(row):
        block = state[row]
        inside = jnp.where(sub2 < species, jnp.broadcast_to(block[2:3], block.shape), 0.0)
        speed_rows = jnp.broadcast_to(block[0:1], block.shape)
        speed_cols = jnp.broadcast_to(block[1:2], block.shape)
        coef_u[row] = inside * (jnp.maximum(speed_rows, 0.0) + spread)
        coef_d[row] = inside * (spread - jnp.minimum(speed_rows, 0.0))
        coef_l[row] = inside * (jnp.maximum(speed_cols, 0.0) + spread)
        coef_r[row] = inside * (spread - jnp.minimum(speed_cols, 0.0))
        coef_c[row] = 1.0 - inside * (
            jnp.abs(speed_rows) + jnp.abs(speed_cols) + 4.0 * spread
        )

    @pl.loop(0, rows)
    def _(row):
        flags = jnp.broadcast_to(live[pl.ds(row, 1), :], (SLOTS, cols))
        state[HALO + row, :, 0:cols] = jnp.where(sub == species + 1, flags, base_ref[row])

    other[...] = jnp.zeros_like(other)
    start(1)
    finish(1, None)

    def substep(source, target):
        @pl.loop(0, (full - 2) // GROUP)
        def _(group):
            row = 1 + group * GROUP
            here = pl.ds(row, GROUP)
            centre = source[here]
            target[here] = (
                coef_c[here] * centre
                + coef_u[here] * source[pl.ds(row - 1, GROUP)]
                + coef_d[here] * source[pl.ds(row + 1, GROUP)]
                + coef_l[here] * pltpu.roll(centre, 1, axis=2)
                + coef_r[here] * pltpu.roll(centre, 2 * cols - 1, axis=2)
            )

    @pl.loop(0, COUPLINGS)
    def _(step):
        for at in range(SUBSTEPS):
            source, target = (state, other) if at % 2 == 0 else (other, state)
            substep(source, target)
        slot = lax.rem(step, 2)
        start(slot)

        @pl.loop(0, rows // CHUNK)
        def _(piece):
            first = HALO + piece * CHUNK
            blocks = react([state[first + at, :, 0:cols] for at in range(CHUNK)])
            for at in range(CHUNK):
                state[first + at, :, 0:cols] = blocks[at]

        finish(slot, react)

    out_ref[...] = state[HALO : HALO + rows, :, 0:cols]


def split_bias(bias):
    high = lax.reduce_precision(bias, 8, 7)
    return jnp.stack([high, bias - high], axis=1).astype(jnp.bfloat16)


def per_device(
    concentration, velocity, solid_fraction, diffusivity, voxel_index, voxel_counts,
    in_weight, in_bias, mid_weight, mid_bias, out_weight, out_bias,
):
    species, rows, cols = concentration.shape
    hidden = mid_weight.shape[0]
    base = jnp.concatenate(
        [
            jnp.transpose(concentration, (1, 0, 2)),
            solid_fraction[:, None, :],
            jnp.zeros((rows, 1, cols), jnp.float32),
            jnp.ones((rows, SLOTS - species - 2, cols), jnp.float32),
        ],
        axis=1,
    )
    shares = jnp.pad(diffusivity, (0, SLOTS - species))[:, None]
    w1 = jnp.concatenate(
        [in_weight.T, jnp.zeros((hidden, 1), jnp.bfloat16), split_bias(in_bias)], axis=1
    )
    gap = jnp.zeros((hidden, SLOTS - 2), jnp.bfloat16)
    w2 = jnp.concatenate([mid_weight.T, split_bias(mid_bias), gap], axis=1)
    w3 = jnp.concatenate([out_weight.T, split_bias(out_bias), gap[:species]], axis=1)
    w3 = jnp.pad(w3, ((0, SLOTS - species), (0, 0)))
    full = rows + 2 * HALO
    tiles = rows * 2 * HALO // cols
    sizes = [lax.axis_size(name) for name in ("gx", "gy", "ga")]

    def body(*refs):
        kernel(rows, cols, species, *sizes, *refs)

    whole = pltpu.VMEM((full, SLOTS, 2 * cols), jnp.float32)
    result = pl.pallas_call(
        body,
        out_shape=jax.ShapeDtypeStruct((rows, SLOTS, cols), jnp.float32),
        in_specs=[pl.BlockSpec(memory_space=pltpu.VMEM)] * 8,
        out_specs=pl.BlockSpec(memory_space=pltpu.VMEM),
        scratch_shapes=[whole] * 7
        + [
            pltpu.VMEM((rows, cols), jnp.float32),
            pltpu.VMEM((tiles, SLOTS, cols), jnp.float32),
            pltpu.VMEM((HALO, SLOTS, cols), jnp.float32),
            pltpu.VMEM((HALO, SLOTS, cols), jnp.float32),
            pltpu.VMEM((2, tiles, SLOTS, cols), jnp.float32),
            pltpu.VMEM((2, tiles, SLOTS, cols), jnp.float32),
            pltpu.VMEM((2, HALO, SLOTS, cols), jnp.float32),
            pltpu.VMEM((2, HALO, SLOTS, cols), jnp.float32),
            pltpu.VMEM((2, 4, SLOTS, cols), jnp.float32),
            pltpu.SemaphoreType.DMA((8,)),
            pltpu.SemaphoreType.DMA((2, 8)),
        ],
        compiler_params=pltpu.CompilerParams(
            collective_id=0, has_side_effects=True, vmem_limit_bytes=48 << 20
        ),
    )(base, velocity, shares, voxel_index, voxel_counts, w1, w2, w3)
    return jnp.transpose(result[:, :species, :], (1, 0, 2))


def solution(mesh):
    tile = P(None, "gx", ("gy", "ga"))
    return jax.shard_map(
        per_device,
        mesh=mesh,
        in_specs=(
            tile, tile, P("gx", ("gy", "ga")), P(),
            P(("gx", "gy", "ga"), None), P("gx", None),
            P(), P(), P(), P(), P(), P(),
        ),
        out_specs=tile,
        check_vma=False,
    )
```

```python
import jax
import jax.numpy as jnp
from jax import lax
from jax.experimental import pallas as pl
from jax.experimental.pallas import tpu as pltpu
from jax.sharding import PartitionSpec as P

SUBSTEPS = 4
COUPLINGS = 16
HALO = SUBSTEPS
SLOTS = 16
CHUNK = 8
GROUP = 70
MESH = pl.DeviceIdType.MESH


def kernel(
    rows, cols, species, gx_count, gy_count, ga_count,
    base_ref, vel_ref, diff_ref, index_ref, counts_ref, w1_ref, w2_ref, w3_ref,
    out_ref,
    state, other, coef_c, coef_u, coef_d, coef_l, coef_r, live,
    edge_out, top_out, bottom_out,
    from_left, from_right, from_up, from_down, from_corner,
    send_sem, recv_sem,
):
    full = rows + 2 * HALO
    width = 2 * HALO
    per_tile = cols // width
    tiles = rows // per_tile
    gx = lax.axis_index("gx")
    gy = lax.axis_index("gy")
    ga = lax.axis_index("ga")
    place = gy * ga_count + ga
    places = gy_count * ga_count

    def device(dx, dp):
        other_place = jnp.clip(place + dp, 0, places - 1)
        return (
            jnp.clip(gx + dx, 0, gx_count - 1),
            lax.div(other_place, ga_count),
            lax.rem(other_place, ga_count),
        )

    has_up, has_down = gx > 0, gx < gx_count - 1
    has_left, has_right = place > 0, place < places - 1
    links = (
        (device(0, -1), has_left),
        (device(0, 1), has_right),
        (device(-1, 0), has_up),
        (device(1, 0), has_down),
        (device(-1, -1), has_up & has_left),
        (device(1, 1), has_down & has_right),
        (device(-1, 1), has_up & has_right),
        (device(1, -1), has_down & has_left),
    )

    for ref in (from_left, from_right, from_up, from_down, from_corner):
        ref[...] = jnp.zeros_like(ref)

    barrier = pltpu.get_barrier_semaphore()
    total = jnp.int32(0)
    for target, exists in links:
        total = total + exists.astype(jnp.int32)

        @pl.when(exists)
        def _():
            pl.semaphore_signal(barrier, inc=1, device_id=target, device_id_type=MESH)

    pl.semaphore_wait(barrier, total)

    lane = lax.broadcasted_iota(jnp.int32, (SLOTS, cols), 1)
    sub = lax.broadcasted_iota(jnp.int32, (SLOTS, cols), 0)
    first_half = lax.rem(lane, width) < HALO

    def copies(slot):
        last = tiles - 1
        plan = (
            (edge_out, from_right.at[slot]),
            (edge_out, from_left.at[slot]),
            (top_out, from_down.at[slot]),
            (bottom_out, from_up.at[slot]),
            (edge_out.at[0], from_corner.at[slot, 3]),
            (edge_out.at[last], from_corner.at[slot, 0]),
            (edge_out.at[0], from_corner.at[slot, 2]),
            (edge_out.at[last], from_corner.at[slot, 1]),
        )
        result = []
        for at, ((source, target_ref), (target, exists)) in enumerate(zip(plan, links)):
            result.append((
                pltpu.make_async_remote_copy(
                    src_ref=source, dst_ref=target_ref,
                    send_sem=send_sem.at[at], recv_sem=recv_sem.at[slot, at],
                    device_id=target, device_id_type=MESH,
                ),
                exists,
            ))
        return result

    def start(slot):
        for tile in range(tiles):
            packed = jnp.zeros((SLOTS, cols), jnp.float32)
            for at in range(per_tile):
                row = state[HALO + tile * per_tile + at, :, 0:cols]
                moved = pltpu.roll(row, (width * at + HALO) % cols, axis=1)
                packed = moved if at == 0 else jnp.where(lane >= width * at, moved, packed)
            edge_out[tile] = packed
        top_out[...] = state[HALO : 2 * HALO, :, 0:cols]
        bottom_out[...] = state[rows : rows + HALO, :, 0:cols]
        for copy, exists in copies(slot):

            @pl.when(exists)
            def _():
                copy.start()

    def finish(slot, change):
        moves = copies(slot)
        for at, (copy, exists) in enumerate(moves):

            @pl.when(exists)
            def _():
                copy.wait_send()

            @pl.when(links[at ^ 1][1])
            def _():
                moves[at][0].wait_recv()

        edges = [
            jnp.where(first_half, from_left[slot, tile], from_right[slot, tile])
            for tile in range(tiles)
        ]
        corner_up = jnp.where(first_half, from_corner[slot, 0], from_corner[slot, 1])
        corner_down = jnp.where(first_half, from_corner[slot, 2], from_corner[slot, 3])
        corner = jnp.where(lane < width * HALO, corner_down, corner_up)
        blocks = edges + [corner]
        blocks += [from_up[slot, at] for at in range(HALO)]
        blocks += [from_down[slot, at] for at in range(HALO)]
        if change is not None:
            blocks = change(blocks)
        corner = blocks[tiles]
        for at in range(HALO):
            state[at, :, 0:cols] = blocks[tiles + 1 + at]
            state[HALO + rows + at, :, 0:cols] = blocks[tiles + 1 + HALO + at]
            window = per_tile - HALO + at
            state[at, :, cols : 2 * cols] = pltpu.roll(
                corner, (2 * cols - width * window - HALO) % cols, axis=1
            )
            state[HALO + rows + at, :, cols : 2 * cols] = pltpu.roll(
                corner, (2 * cols - width * at - HALO) % cols, axis=1
            )
        for tile in range(tiles):
            for at in range(per_tile):
                state[HALO + tile * per_tile + at, :, cols : 2 * cols] = pltpu.roll(
                    blocks[tile], (2 * cols - width * at - HALO) % cols, axis=1
                )

    def react(blocks):
        count = len(blocks)
        features = jnp.concatenate([block.astype(jnp.bfloat16) for block in blocks], axis=1)
        ones = jnp.ones((SLOTS, count * cols), jnp.bfloat16)
        hidden = jnp.dot(w1_ref[...], features, preferred_element_type=jnp.float32)
        hidden = jnp.tanh(hidden).astype(jnp.bfloat16)
        hidden = jnp.concatenate([hidden, ones], axis=0)
        hidden = jnp.dot(w2_ref[...], hidden, preferred_element_type=jnp.float32)
        hidden = jnp.tanh(hidden).astype(jnp.bfloat16)
        hidden = jnp.concatenate([hidden, ones], axis=0)
        gain = jnp.dot(w3_ref[...], hidden, preferred_element_type=jnp.float32)
        gain = gain.astype(jnp.bfloat16).astype(jnp.float32)
        return [
            block
            + jnp.where(
                jnp.broadcast_to(block[species + 1 : species + 2], block.shape) > 1.5,
                gain[:, at * cols : (at + 1) * cols],
                0.0,
            )
            for at, block in enumerate(blocks)
        ]

    candidates = index_ref[...]
    counts = counts_ref[...]
    own = lax.broadcasted_iota(jnp.int32, counts.shape, 1) == place
    own_count = jnp.sum(jnp.where(own, counts, 0), axis=1, keepdims=True)
    entry = lax.broadcasted_iota(jnp.int32, candidates.shape, 1)
    candidates = jnp.where(entry < own_count, candidates, -1)
    cell_row = jnp.right_shift(candidates, cols.bit_length() - 1)
    cell_col = jnp.bitwise_and(candidates, cols - 1)
    entries = candidates.shape[1]
    row_at = lax.broadcasted_iota(jnp.int32, (rows, entries), 0)
    col_at = lax.broadcasted_iota(jnp.int32, (cols, entries), 0)
    row_hot = jnp.where(row_at == cell_row, 1.0, 0.0).astype(jnp.bfloat16)
    col_hot = jnp.where(col_at == cell_col, 1.0, 0.0).astype(jnp.bfloat16)
    live[...] = lax.dot_general(
        row_hot, col_hot, (((1,), (1,)), ((), ())), preferred_element_type=jnp.float32
    )

    @pl.loop(0, rows)
    def _(row):
        flags = 1.0 + jnp.broadcast_to(live[pl.ds(row, 1), :], (SLOTS, cols))
        speed_rows = jnp.broadcast_to(vel_ref[0, pl.ds(row, 1), :], (SLOTS, cols))
        speed_cols = jnp.broadcast_to(vel_ref[1, pl.ds(row, 1), :], (SLOTS, cols))
        block = jnp.where(sub == species + 1, flags, base_ref[row])
        block = jnp.where(sub == species + 2, speed_rows, block)
        state[HALO + row, :, 0:cols] = jnp.where(sub == species + 3, speed_cols, block)

    start(0)
    other[...] = jnp.zeros_like(other)
    finish(0, None)
    sub2 = lax.broadcasted_iota(jnp.int32, (SLOTS, 2 * cols), 0)
    spread = jnp.broadcast_to(diff_ref[...], (SLOTS, 2 * cols))

    @pl.loop(0, full)
    def _(row):
        block = state[row]
        inside = jnp.minimum(jnp.broadcast_to(block[species + 1 : species + 2], block.shape), 1.0)
        inside = jnp.where(sub2 < species, inside, 0.0)
        speed_rows = jnp.broadcast_to(block[species + 2 : species + 3], block.shape)
        speed_cols = jnp.broadcast_to(block[species + 3 : species + 4], block.shape)
        coef_u[row] = inside * (jnp.maximum(speed_rows, 0.0) + spread)
        coef_d[row] = inside * (spread - jnp.minimum(speed_rows, 0.0))
        coef_l[row] = inside * (jnp.maximum(speed_cols, 0.0) + spread)
        coef_r[row] = inside * (spread - jnp.minimum(speed_cols, 0.0))
        coef_c[row] = 1.0 - inside * (
            jnp.abs(speed_rows) + jnp.abs(speed_cols) + 4.0 * spread
        )
        state[row] = jnp.where(sub2 < species + 2, block, 1.0)

    def substep(source, target):
        @pl.loop(0, (full - 2) // GROUP)
        def _(group):
            row = 1 + group * GROUP
            here = pl.ds(row, GROUP)
            centre = source[here]
            target[here] = (
                coef_c[here] * centre
                + coef_u[here] * source[pl.ds(row - 1, GROUP)]
                + coef_d[here] * source[pl.ds(row + 1, GROUP)]
                + coef_l[here] * pltpu.roll(centre, 1, axis=2)
                + coef_r[here] * pltpu.roll(centre, 2 * cols - 1, axis=2)
            )

    @pl.loop(0, COUPLINGS)
    def _(step):
        for at in range(SUBSTEPS):
            source, target = (state, other) if at % 2 == 0 else (other, state)
            substep(source, target)
        slot = lax.rem(step + 1, 2)

        @pl.when(step < COUPLINGS - 1)
        def _():
            start(slot)

        @pl.loop(0, rows // CHUNK)
        def _(piece):
            first = HALO + piece * CHUNK
            blocks = react([state[first + at, :, 0:cols] for at in range(CHUNK)])
            for at in range(CHUNK):
                state[first + at, :, 0:cols] = blocks[at]

        @pl.when(step < COUPLINGS - 1)
        def _():
            finish(slot, react)

    out_ref[...] = state[HALO : HALO + rows, :, 0:cols]


def split_bias(bias):
    high = lax.reduce_precision(bias, 8, 7)
    return jnp.stack([high, bias - high], axis=1).astype(jnp.bfloat16)


def per_device(
    concentration, velocity, solid_fraction, diffusivity, voxel_index, voxel_counts,
    in_weight, in_bias, mid_weight, mid_bias, out_weight, out_bias,
):
    species, rows, cols = concentration.shape
    hidden = mid_weight.shape[0]
    base = jnp.concatenate(
        [
            jnp.transpose(concentration, (1, 0, 2)),
            solid_fraction[:, None, :],
            jnp.zeros((rows, 1, cols), jnp.float32),
            jnp.ones((rows, SLOTS - species - 2, cols), jnp.float32),
        ],
        axis=1,
    )
    shares = jnp.pad(diffusivity, (0, SLOTS - species))[:, None]
    w1 = jnp.concatenate(
        [in_weight.T, jnp.zeros((hidden, 1), jnp.bfloat16), split_bias(in_bias)], axis=1
    )
    gap = jnp.zeros((hidden, SLOTS - 2), jnp.bfloat16)
    w2 = jnp.concatenate([mid_weight.T, split_bias(mid_bias), gap], axis=1)
    w3 = jnp.concatenate([out_weight.T, split_bias(out_bias), gap[:species]], axis=1)
    w3 = jnp.pad(w3, ((0, SLOTS - species), (0, 0)))
    full = rows + 2 * HALO
    tiles = rows * 2 * HALO // cols
    sizes = [lax.axis_size(name) for name in ("gx", "gy", "ga")]

    def body(*refs):
        kernel(rows, cols, species, *sizes, *refs)

    whole = pltpu.VMEM((full, SLOTS, 2 * cols), jnp.float32)
    result = pl.pallas_call(
        body,
        out_shape=jax.ShapeDtypeStruct((rows, SLOTS, cols), jnp.float32),
        in_specs=[pl.BlockSpec(memory_space=pltpu.VMEM)] * 8,
        out_specs=pl.BlockSpec(memory_space=pltpu.VMEM),
        scratch_shapes=[whole] * 7
        + [
            pltpu.VMEM((rows, cols), jnp.float32),
            pltpu.VMEM((tiles, SLOTS, cols), jnp.float32),
            pltpu.VMEM((HALO, SLOTS, cols), jnp.float32),
            pltpu.VMEM((HALO, SLOTS, cols), jnp.float32),
            pltpu.VMEM((2, tiles, SLOTS, cols), jnp.float32),
            pltpu.VMEM((2, tiles, SLOTS, cols), jnp.float32),
            pltpu.VMEM((2, HALO, SLOTS, cols), jnp.float32),
            pltpu.VMEM((2, HALO, SLOTS, cols), jnp.float32),
            pltpu.VMEM((2, 4, SLOTS, cols), jnp.float32),
            pltpu.SemaphoreType.DMA((8,)),
            pltpu.SemaphoreType.DMA((2, 8)),
        ],
        compiler_params=pltpu.CompilerParams(
            collective_id=0, has_side_effects=True, vmem_limit_bytes=48 << 20
        ),
    )(base, velocity, shares, voxel_index, voxel_counts, w1, w2, w3)
    return jnp.transpose(result[:, :species, :], (1, 0, 2))


def solution(mesh):
    tile = P(None, "gx", ("gy", "ga"))
    return jax.shard_map(
        per_device,
        mesh=mesh,
        in_specs=(
            tile, tile, P("gx", ("gy", "ga")), P(),
            P(("gx", "gy", "ga"), None), P("gx", None),
            P(), P(), P(), P(), P(), P(),
        ),
        out_specs=tile,
        check_vma=False,
    )
```

```python
import jax
import jax.numpy as jnp
from jax import lax
from jax.experimental import pallas as pl
from jax.experimental.pallas import tpu as pltpu
from jax.sharding import PartitionSpec as P

SUBSTEPS = 4
COUPLINGS = 16
HALO = SUBSTEPS
SLOTS = 16
CHUNK = 8
MESH = pl.DeviceIdType.MESH


def kernel(
    rows, cols, species, gx_count, gy_count, ga_count,
    base_ref, vel_ref, diff_ref, index_ref, counts_ref, w1_ref, w2_ref, w3_ref,
    out_ref,
    state, other, coef_c, coef_u, coef_d, coef_l, coef_r, live,
    edge_out, top_out, bottom_out,
    from_left, from_right, from_up, from_down, from_corner,
    send_sem, recv_sem,
):
    full = rows + 2 * HALO
    width = 2 * HALO
    per_tile = cols // width
    tiles = rows // per_tile
    gx = lax.axis_index("gx")
    gy = lax.axis_index("gy")
    ga = lax.axis_index("ga")
    place = gy * ga_count + ga
    places = gy_count * ga_count

    def device(dx, dp):
        other_place = jnp.clip(place + dp, 0, places - 1)
        return (
            jnp.clip(gx + dx, 0, gx_count - 1),
            lax.div(other_place, ga_count),
            lax.rem(other_place, ga_count),
        )

    has_up, has_down = gx > 0, gx < gx_count - 1
    has_left, has_right = place > 0, place < places - 1
    links = (
        (device(0, -1), has_left),
        (device(0, 1), has_right),
        (device(-1, 0), has_up),
        (device(1, 0), has_down),
        (device(-1, -1), has_up & has_left),
        (device(1, 1), has_down & has_right),
        (device(-1, 1), has_up & has_right),
        (device(1, -1), has_down & has_left),
    )

    for ref in (from_left, from_right, from_up, from_down, from_corner):
        ref[...] = jnp.zeros_like(ref)

    barrier = pltpu.get_barrier_semaphore()
    total = jnp.int32(0)
    for target, exists in links:
        total = total + exists.astype(jnp.int32)

        @pl.when(exists)
        def _():
            pl.semaphore_signal(barrier, inc=1, device_id=target, device_id_type=MESH)

    pl.semaphore_wait(barrier, total)

    lane = lax.broadcasted_iota(jnp.int32, (SLOTS, cols), 1)
    sub = lax.broadcasted_iota(jnp.int32, (SLOTS, cols), 0)
    first_half = lax.rem(lane, width) < HALO

    def copies(slot):
        last = tiles - 1
        plan = (
            (edge_out, from_right.at[slot]),
            (edge_out, from_left.at[slot]),
            (top_out, from_down.at[slot]),
            (bottom_out, from_up.at[slot]),
            (edge_out.at[0], from_corner.at[slot, 3]),
            (edge_out.at[last], from_corner.at[slot, 0]),
            (edge_out.at[0], from_corner.at[slot, 2]),
            (edge_out.at[last], from_corner.at[slot, 1]),
        )
        result = []
        for at, ((source, target_ref), (target, exists)) in enumerate(zip(plan, links)):
            result.append((
                pltpu.make_async_remote_copy(
                    src_ref=source, dst_ref=target_ref,
                    send_sem=send_sem.at[at], recv_sem=recv_sem.at[slot, at],
                    device_id=target, device_id_type=MESH,
                ),
                exists,
            ))
        return result

    def start(slot):
        for tile in range(tiles):
            packed = jnp.zeros((SLOTS, cols), jnp.float32)
            for at in range(per_tile):
                row = state[HALO + tile * per_tile + at, :, 0:cols]
                moved = pltpu.roll(row, (width * at + HALO) % cols, axis=1)
                packed = moved if at == 0 else jnp.where(lane >= width * at, moved, packed)
            edge_out[tile] = packed
        top_out[...] = state[HALO : 2 * HALO, :, 0:cols]
        bottom_out[...] = state[rows : rows + HALO, :, 0:cols]
        for copy, exists in copies(slot):

            @pl.when(exists)
            def _():
                copy.start()

    def finish(slot, change):
        moves = copies(slot)
        for at, (copy, exists) in enumerate(moves):

            @pl.when(exists)
            def _():
                copy.wait_send()

            @pl.when(links[at ^ 1][1])
            def _():
                moves[at][0].wait_recv()

        edges = [
            jnp.where(first_half, from_left[slot, tile], from_right[slot, tile])
            for tile in range(tiles)
        ]
        corner_up = jnp.where(first_half, from_corner[slot, 0], from_corner[slot, 1])
        corner_down = jnp.where(first_half, from_corner[slot, 2], from_corner[slot, 3])
        corner = jnp.where(lane < width * HALO, corner_down, corner_up)
        blocks = edges + [corner]
        blocks += [from_up[slot, at] for at in range(HALO)]
        blocks += [from_down[slot, at] for at in range(HALO)]
        if change is not None:
            blocks = change(blocks)
        corner = blocks[tiles]
        for at in range(HALO):
            state[at, :, 0:cols] = blocks[tiles + 1 + at]
            state[HALO + rows + at, :, 0:cols] = blocks[tiles + 1 + HALO + at]
            window = per_tile - HALO + at
            state[at, :, cols : 2 * cols] = pltpu.roll(
                corner, (2 * cols - width * window - HALO) % cols, axis=1
            )
            state[HALO + rows + at, :, cols : 2 * cols] = pltpu.roll(
                corner, (2 * cols - width * at - HALO) % cols, axis=1
            )
        for tile in range(tiles):
            for at in range(per_tile):
                state[HALO + tile * per_tile + at, :, cols : 2 * cols] = pltpu.roll(
                    blocks[tile], (2 * cols - width * at - HALO) % cols, axis=1
                )

    def react(blocks):
        count = len(blocks)
        features = jnp.concatenate([block.astype(jnp.bfloat16) for block in blocks], axis=1)
        ones = jnp.ones((SLOTS, count * cols), jnp.bfloat16)
        hidden = jnp.dot(w1_ref[...], features, preferred_element_type=jnp.float32)
        hidden = jnp.tanh(hidden).astype(jnp.bfloat16)
        hidden = jnp.concatenate([hidden, ones], axis=0)
        hidden = jnp.dot(w2_ref[...], hidden, preferred_element_type=jnp.float32)
        hidden = jnp.tanh(hidden).astype(jnp.bfloat16)
        hidden = jnp.concatenate([hidden, ones], axis=0)
        gain = jnp.dot(w3_ref[...], hidden, preferred_element_type=jnp.float32)
        gain = gain.astype(jnp.bfloat16).astype(jnp.float32)
        return [
            block
            + jnp.where(
                jnp.broadcast_to(block[species + 1 : species + 2], block.shape) > 1.5,
                gain[:, at * cols : (at + 1) * cols],
                0.0,
            )
            for at, block in enumerate(blocks)
        ]

    candidates = index_ref[...]
    counts = counts_ref[...]
    own = lax.broadcasted_iota(jnp.int32, counts.shape, 1) == place
    own_count = jnp.sum(jnp.where(own, counts, 0), axis=1, keepdims=True)
    entry = lax.broadcasted_iota(jnp.int32, candidates.shape, 1)
    candidates = jnp.where(entry < own_count, candidates, -1)
    cell_row = jnp.right_shift(candidates, cols.bit_length() - 1)
    cell_col = jnp.bitwise_and(candidates, cols - 1)
    entries = candidates.shape[1]
    row_at = lax.broadcasted_iota(jnp.int32, (rows, entries), 0)
    col_at = lax.broadcasted_iota(jnp.int32, (cols, entries), 0)
    row_hot = jnp.where(row_at == cell_row, 1.0, 0.0).astype(jnp.bfloat16)
    col_hot = jnp.where(col_at == cell_col, 1.0, 0.0).astype(jnp.bfloat16)
    live[...] = lax.dot_general(
        row_hot, col_hot, (((1,), (1,)), ((), ())), preferred_element_type=jnp.float32
    )

    @pl.loop(0, rows)
    def _(row):
        flags = 1.0 + jnp.broadcast_to(live[pl.ds(row, 1), :], (SLOTS, cols))
        speed_rows = jnp.broadcast_to(vel_ref[0, pl.ds(row, 1), :], (SLOTS, cols))
        speed_cols = jnp.broadcast_to(vel_ref[1, pl.ds(row, 1), :], (SLOTS, cols))
        block = jnp.where(sub == species + 1, flags, base_ref[row])
        block = jnp.where(sub == species + 2, speed_rows, block)
        state[HALO + row, :, 0:cols] = jnp.where(sub == species + 3, speed_cols, block)

    start(0)
    finish(0, None)
    sub2 = lax.broadcasted_iota(jnp.int32, (SLOTS, 2 * cols), 0)
    spread = jnp.broadcast_to(diff_ref[...], (SLOTS, 2 * cols))

    @pl.loop(0, full)
    def _(row):
        block = state[row]
        inside = jnp.minimum(jnp.broadcast_to(block[species + 1 : species + 2], block.shape), 1.0)
        inside = jnp.where(sub2 < species, inside, 0.0)
        speed_rows = jnp.broadcast_to(block[species + 2 : species + 3], block.shape)
        speed_cols = jnp.broadcast_to(block[species + 3 : species + 4], block.shape)
        coef_u[row] = inside * (jnp.maximum(speed_rows, 0.0) + spread)
        coef_d[row] = inside * (spread - jnp.minimum(speed_rows, 0.0))
        coef_l[row] = inside * (jnp.maximum(speed_cols, 0.0) + spread)
        coef_r[row] = inside * (spread - jnp.minimum(speed_cols, 0.0))
        coef_c[row] = 1.0 - inside * (
            jnp.abs(speed_rows) + jnp.abs(speed_cols) + 4.0 * spread
        )
        state[row] = jnp.where(sub2 < species + 2, block, 1.0)

    def substep(source, target, low, high):
        here = pl.ds(low, high - low)
        centre = source[here]
        target[here] = (
            coef_c[here] * centre
            + coef_u[here] * source[pl.ds(low - 1, high - low)]
            + coef_d[here] * source[pl.ds(low + 1, high - low)]
            + coef_l[here] * pltpu.roll(centre, 1, axis=2)
            + coef_r[here] * pltpu.roll(centre, 2 * cols - 1, axis=2)
        )

    @pl.loop(0, COUPLINGS)
    def _(step):
        for at in range(SUBSTEPS):
            source, target = (state, other) if at % 2 == 0 else (other, state)
            substep(source, target, at + 1, full - 1 - at)
        slot = lax.rem(step + 1, 2)

        @pl.when(step < COUPLINGS - 1)
        def _():
            start(slot)

        @pl.loop(0, rows // CHUNK)
        def _(piece):
            first = HALO + piece * CHUNK
            blocks = react([state[first + at, :, 0:cols] for at in range(CHUNK)])
            for at in range(CHUNK):
                state[first + at, :, 0:cols] = blocks[at]

        @pl.when(step < COUPLINGS - 1)
        def _():
            finish(slot, react)

    out_ref[...] = state[HALO : HALO + rows, :, 0:cols]


def split_bias(bias):
    high = lax.reduce_precision(bias, 8, 7)
    return jnp.stack([high, bias - high], axis=1).astype(jnp.bfloat16)


def per_device(
    concentration, velocity, solid_fraction, diffusivity, voxel_index, voxel_counts,
    in_weight, in_bias, mid_weight, mid_bias, out_weight, out_bias,
):
    species, rows, cols = concentration.shape
    hidden = mid_weight.shape[0]
    base = jnp.concatenate(
        [
            jnp.transpose(concentration, (1, 0, 2)),
            solid_fraction[:, None, :],
            jnp.zeros((rows, 1, cols), jnp.float32),
            jnp.ones((rows, SLOTS - species - 2, cols), jnp.float32),
        ],
        axis=1,
    )
    shares = jnp.pad(diffusivity, (0, SLOTS - species))[:, None]
    w1 = jnp.concatenate(
        [in_weight.T, jnp.zeros((hidden, 1), jnp.bfloat16), split_bias(in_bias)], axis=1
    )
    gap = jnp.zeros((hidden, SLOTS - 2), jnp.bfloat16)
    w2 = jnp.concatenate([mid_weight.T, split_bias(mid_bias), gap], axis=1)
    w3 = jnp.concatenate([out_weight.T, split_bias(out_bias), gap[:species]], axis=1)
    w3 = jnp.pad(w3, ((0, SLOTS - species), (0, 0)))
    full = rows + 2 * HALO
    tiles = rows * 2 * HALO // cols
    sizes = [lax.axis_size(name) for name in ("gx", "gy", "ga")]

    def body(*refs):
        kernel(rows, cols, species, *sizes, *refs)

    whole = pltpu.VMEM((full, SLOTS, 2 * cols), jnp.float32)
    result = pl.pallas_call(
        body,
        out_shape=jax.ShapeDtypeStruct((rows, SLOTS, cols), jnp.float32),
        in_specs=[pl.BlockSpec(memory_space=pltpu.VMEM)] * 8,
        out_specs=pl.BlockSpec(memory_space=pltpu.VMEM),
        scratch_shapes=[whole] * 7
        + [
            pltpu.VMEM((rows, cols), jnp.float32),
            pltpu.VMEM((tiles, SLOTS, cols), jnp.float32),
            pltpu.VMEM((HALO, SLOTS, cols), jnp.float32),
            pltpu.VMEM((HALO, SLOTS, cols), jnp.float32),
            pltpu.VMEM((2, tiles, SLOTS, cols), jnp.float32),
            pltpu.VMEM((2, tiles, SLOTS, cols), jnp.float32),
            pltpu.VMEM((2, HALO, SLOTS, cols), jnp.float32),
            pltpu.VMEM((2, HALO, SLOTS, cols), jnp.float32),
            pltpu.VMEM((2, 4, SLOTS, cols), jnp.float32),
            pltpu.SemaphoreType.DMA((8,)),
            pltpu.SemaphoreType.DMA((2, 8)),
        ],
        compiler_params=pltpu.CompilerParams(
            collective_id=0, has_side_effects=True, vmem_limit_bytes=48 << 20
        ),
    )(base, velocity, shares, voxel_index, voxel_counts, w1, w2, w3)
    return jnp.transpose(result[:, :species, :], (1, 0, 2))


def solution(mesh):
    tile = P(None, "gx", ("gy", "ga"))
    return jax.shard_map(
        per_device,
        mesh=mesh,
        in_specs=(
            tile, tile, P("gx", ("gy", "ga")), P(),
            P(("gx", "gy", "ga"), None), P("gx", None),
            P(), P(), P(), P(), P(), P(),
        ),
        out_specs=tile,
        check_vma=False,
    )
```
